32 devices in a mesh: gy: 16 (over z, y, core), gz: 2 (over x).
Axes of the slice: x: 2, y: 2, z: 4, core: 2. Of those that a mesh axis runs over, the one named last changes fastest.
Arguments:
- initial_block: bfloat16 [16, 2, 2, 512, 512], P('gy', 'gz'), may hold values from -6 to 6
- tile_ops: bfloat16 [16, 2, 2, 512, 512], P('gy', 'gz'), may hold values from -0.125 to 0.125
- couple_ops: bfloat16 [16, 2, 4, 2, 512, 512], P('gy', 'gz'), may hold values from -0.125 to 0.125
- couple_map: int32 [16, 2, 4, 2], P('gy', 'gz'), may hold values from 0 to 1
- cell_scale: float32 [16, 2, 2, 512], P('gy', 'gz'), may hold values from 0.4 to 2.5
Outputs:
- basis: float32 [16, 2, 2, 512, 512], P('gy', 'gz')
- factor: float32 [512, 512], replicated
The draws below stay inside these ranges and needn't reach their ends.
All inputs are finite; a program needn't handle non-finite values.
Results may differ from the reference program's by a relative error of at most 0.0053.
Values may be sent and summed in bfloat16 or wider, within the bound.
A program may use at most 64 MiB of HBM per device.

```python
import math
import jax
import jax.numpy as jnp
from jax import lax

TILE = 512
VECS = 512
TILES = 2
CELLS = 32768
N_GY = 16
N_GZ = 2


def place_ends(result, rng, smallest, largest):
    longest = result.shape.index(max(result.shape))
    spots = []
    for shift in (0, 1):
        where = [jax.random.randint(jax.random.fold_in(rng, axis), (), 0, length) for axis, length in enumerate(result.shape)]
        where[longest] = (where[longest] + shift) % result.shape[longest]
        spots.append(tuple(where))
    return result.at[spots[0]].set(smallest).at[spots[1]].set(largest)


def block_levels(rng, dims, split, least, largest):
    loudness = 1.0
    for axis_at, blocks in split:
        heights = jax.random.uniform(jax.random.fold_in(jax.random.fold_in(rng, 6), axis_at), (blocks,), jnp.float32, least / len(split), largest / len(split))
        loudness = loudness * jnp.repeat(jnp.exp(heights), dims[axis_at] // blocks).reshape((-1,) + (1,) * (len(dims) - 1 - axis_at))
    return loudness


def gaussian(own_key, dims, scale, bound, shards=(), kind=jnp.bfloat16):
    loudness = block_levels(own_key, dims, shards, -0.22, 0.18) if shards else 1.0
    result = jax.random.normal(own_key, dims, jnp.float32) * scale * loudness
    return jnp.minimum(jnp.maximum(result, -bound), bound).astype(kind)


def setup_inputs(seed: int = 0) -> dict:
    seeds = jax.random.split(jax.random.key(seed), 6)
    return {
        "initial_block": gaussian(seeds[0], (N_GY, N_GZ, TILES, TILE, VECS), 1.0, 6.0, ((0, 16), (1, 2))),
        "tile_ops": gaussian(seeds[1], (N_GY, N_GZ, TILES, TILE, TILE), (5 * TILE) ** -0.5, 0.125, ((0, 16), (1, 2))),
        "couple_ops": gaussian(seeds[2], (N_GY, N_GZ, 4, TILES, TILE, TILE), (5 * TILE) ** -0.5, 0.125, ((0, 16), (1, 2))),
        "couple_map": place_ends(jax.random.randint(seeds[3], (N_GY, N_GZ, 4, TILES), 0, TILES), jax.random.fold_in(seeds[3], 1), 0, TILES - 1).astype(jnp.int32),
        "cell_scale": jnp.clip(jnp.exp(math.log(2.5) - 1.8325814 * jax.random.uniform(seeds[4], (N_GY, N_GZ, TILES, TILE), jnp.float32) ** block_levels(seeds[4], (N_GY, N_GZ, TILES, TILE), ((0, 16), (1, 2)), -0.2, 0.2)), 0.4, 2.5),
    }


def pick_tiles(blocks, indices):
    return jnp.take(blocks, indices, axis=0)

def apply_scaled(field, tile_ops, couple_ops, couple_map, cell_scale):
    scaled = (cell_scale[..., None] * field).astype(jnp.bfloat16)
    total = jnp.einsum('abtij,abtjk->abtik', tile_ops.astype(jnp.float32), scaled.astype(jnp.float32), precision=lax.Precision.HIGHEST)
    moves = [(1, 0), (-1, 0), (1, 1), (-1, 1)]
    for direction in range(4):
        offset, axis_number = moves[direction]
        beside = jnp.roll(scaled, offset, axis=axis_number)
        picked = jax.vmap(jax.vmap(pick_tiles))(beside, couple_map[:, :, direction])
        total = total + jnp.einsum('abtij,abtjk->abtik', couple_ops[:, :, direction].astype(jnp.float32), picked.astype(jnp.float32), precision=lax.Precision.HIGHEST)
    return cell_scale[..., None] * total

def reference(initial_block, tile_ops, couple_ops, couple_map, cell_scale):

    def filter_map(field):
        return ((1.0 - 1.1) * field - apply_scaled(field, tile_ops, couple_ops, couple_map, cell_scale)) / 0.9
    first = initial_block.astype(jnp.float32)
    second = filter_map(first)
    third = 2.0 * filter_map(second) - first
    fourth = 2.0 * filter_map(third) - second
    flat = fourth.reshape(-1, VECS)
    gram = jnp.einsum('ck,cl->kl', flat, flat, precision=lax.Precision.HIGHEST) / jnp.float32(CELLS)
    lower = jnp.linalg.cholesky(gram)
    basis = jax.scipy.linalg.solve_triangular(lower, flat.T, lower=True).T
    return (basis.reshape(fourth.shape), lower.T)
```

```python
import functools

import jax
import jax.numpy as jnp
from jax import lax
from jax.experimental import pallas as pl
from jax.experimental.pallas import tpu as pltpu
from jax.sharding import PartitionSpec as P

F32, BF16 = jnp.float32, jnp.bfloat16
MESH = pl.DeviceIdType.MESH
ROUNDS = 3
CHUNKS = 2
BASE = 128
PANEL = 8


def split(x):
    hi = x.astype(BF16)
    return hi, (x - hi.astype(F32)).astype(BF16)


def xor_stages(ny, nz, rows):
    order = [("gy", 0)]
    order += [("gz", b) for b in range(nz.bit_length() - 1)]
    order += [("gy", b) for b in range(1, ny.bit_length() - 1)]
    stages, size = [], rows
    for axis, bit in order:
        halve = size % 16 == 0
        stages.append((axis, bit, size, halve))
        size = size // 2 if halve else size
    return stages


def filter_kernel(
    ny, nz, stages, nvec,
    map_ref, scale_ref, first_ref, tile_hbm, couple_hbm,
    y_ref, gram_ref,
    tile_ref, couple_ref, sent, second, third, hi, lo, gsum, gall, *rest,
):
    pieces, rest = rest[: len(stages)], rest[len(stages):]
    op_sem, send_sem, recv_sem, rs_send, rs_recv, ag_send, ag_recv, *landed = rest
    got = {
        (d, r, c): landed[(d * ROUNDS + r) * CHUNKS + c]
        for d in range(len(landed) // (ROUNDS * CHUNKS)) for r in range(ROUNDS) for c in range(CHUNKS)
    }
    tiles, cells, width = first_ref.shape
    cw = width // CHUNKS
    iy, iz = lax.axis_index("gy"), lax.axis_index("gz")
    where = {"gy": iy, "gz": iz}

    def partner(axis, bit):
        me = where[axis]
        b = (me // (2**bit)) % 2
        return {axis: me + (1 - 2 * b) * (2**bit)}, b

    targets = [{"gy": (iy + 1) % ny}, {"gy": (iy + ny - 1) % ny}]
    if nz == 2:
        targets.append({"gz": 1 - iz})
        slot = (0, 1, 2, 2)
    else:
        targets += [{"gz": (iz + 1) % nz}, {"gz": (iz + nz - 1) % nz}]
        slot = (0, 1, 2, 3)

    copies_in = [
        pltpu.make_async_copy(tile_hbm, tile_ref, op_sem.at[0]),
        pltpu.make_async_copy(couple_hbm, couple_ref, op_sem.at[1]),
    ]
    for copy in copies_in:
        copy.start()

    barrier = pltpu.get_barrier_semaphore()
    greeted = targets + [partner(axis, bit)[0] for axis, bit, _, _ in stages]
    for other in greeted:
        pl.semaphore_signal(barrier, inc=1, device_id=other, device_id_type=MESH)

    def send(r, c):
        made = []
        for d, other in enumerate(targets):
            copy = pltpu.make_async_remote_copy(
                src_ref=sent.at[r, c],
                dst_ref=got[d, r, c],
                send_sem=send_sem.at[d, r, c],
                recv_sem=recv_sem.at[d, r, c],
                device_id=other,
                device_id_type=MESH,
            )
            copy.start()
            made.append(copy)
        return made

    moving = {}
    for c in range(CHUNKS):
        for t in range(tiles):
            sent[0, c, t] = (scale_ref[t] * first_ref[t, :, c * cw:(c + 1) * cw].astype(F32)).astype(BF16)
        if c == 0:
            pl.semaphore_wait(barrier, len(greeted))
        moving[0, c] = send(0, c)
    for copy in copies_in:
        copy.wait()

    def gram_of(i, j, place):
        def dot(a, b):
            return lax.dot_general(a, b, (((0,), (0,)), ((), ())), preferred_element_type=F32)
        left, right = slice(i * cw, (i + 1) * cw), slice(j * cw, (j + 1) * cw)
        total = dot(hi[:, left], hi[:, right])
        total += dot(hi[:, left], lo[:, right])
        total += dot(lo[:, left], hi[:, right])
        gsum[place * cw:(place + 1) * cw] = total

    for r in range(ROUNDS):
        for c in range(CHUNKS):
            for copy in moving[r, c]:
                copy.wait_recv()
            cols = slice(c * cw, (c + 1) * cw)

            def one(t, carry, r=r, c=c, cols=cols):
                acc = jnp.dot(tile_ref[t], sent[r, c, t], preferred_element_type=F32)
                for d in range(4):
                    acc += jnp.dot(
                        couple_ref[d, t], got[slot[d], r, c][map_ref[d, t]], preferred_element_type=F32
                    )
                s = scale_ref[t]
                if r == 0:
                    y = first_ref[t, :, cols].astype(F32)
                elif r == 1:
                    y = second[c, t]
                else:
                    y = third[c, t]
                py = ((1.0 - 1.1) * y - s * acc) / 0.9
                if r == 0:
                    new = py
                    second[c, t] = new
                elif r == 1:
                    new = 2.0 * py - first_ref[t, :, cols].astype(F32)
                    third[c, t] = new
                else:
                    new = 2.0 * py - second[c, t]
                    y_ref[t, :, cols] = new
                    a, b = split(new)
                    here = pl.ds(pl.multiple_of(t * cells, cells), cells)
                    hi[here, cols] = a
                    lo[here, cols] = b
                if r < ROUNDS - 1:
                    sent[r + 1, c, t] = (s * new).astype(BF16)
                return carry

            lax.fori_loop(0, tiles, one, 0)
            if r < ROUNDS - 1:
                moving[r + 1, c] = send(r + 1, c)
            else:
                place = c * (c + 1) // 2
                for i in range(c + 1):
                    gram_of(i, c, place + i)

    base = 0
    for n, (axis, bit, size, halve) in enumerate(stages):
        other, b = partner(axis, bit)
        part = size // 2 if halve else size
        out = base + (1 - b) * part if halve else base
        keep = base + b * part if halve else base
        copy = pltpu.make_async_remote_copy(
            src_ref=gsum.at[pl.ds(pl.multiple_of(out, 8), part)],
            dst_ref=pieces[n],
            send_sem=rs_send.at[n],
            recv_sem=rs_recv.at[n],
            device_id=other,
            device_id_type=MESH,
        )
        copy.start()
        copy.wait()
        here = pl.ds(pl.multiple_of(keep, 8), part)
        gsum[here] = gsum[here] + pieces[n][...]
        base = keep
    last = stages[-1][2] // 2 if stages[-1][3] else stages[-1][2]
    here = pl.ds(pl.multiple_of(base, 8), last)
    gall[here] = gsum[here]
    for n in reversed(range(len(stages))):
        axis, bit, size, halve = stages[n]
        if not halve:
            continue
        other, b = partner(axis, bit)
        here = pl.ds(pl.multiple_of(base, 8), size // 2)
        copy = pltpu.make_async_remote_copy(
            src_ref=gall.at[here],
            dst_ref=gall.at[here],
            send_sem=ag_send.at[n],
            recv_sem=ag_recv.at[n],
            device_id=other,
            device_id_type=MESH,
        )
        copy.start()
        copy.wait()
        base = base - b * (size // 2)
    gram_ref[...] = gall[...]
    for made in moving.values():
        for copy in made:
            copy.wait_send()


def factor_block(work):
    sub = lax.broadcasted_iota(jnp.int32, (PANEL, BASE), 0)
    lane = lax.broadcasted_iota(jnp.int32, (PANEL, BASE), 1)

    def panel(p, carry):
        rows = pl.ds(pl.multiple_of(p * PANEL, PANEL), PANEL)
        left, right = work[rows, :BASE], work[rows, BASE:]
        turned = pltpu.roll(left, lax.rem(BASE - p * PANEL, BASE), 1)
        cols = [jnp.broadcast_to(turned[:, j:j + 1], (PANEL, BASE)) for j in range(PANEL)]
        scale = jnp.zeros((PANEL, BASE), F32)
        for i in range(PANEL):
            def row(x):
                return jnp.broadcast_to(x[i:i + 1], (PANEL, BASE))
            inv = lax.rsqrt(row(cols[i]))
            coef = jnp.where(sub > i, cols[i] * (inv * inv), 0.0)
            scale = jnp.where(sub == i, inv, scale)
            for j in range(i + 1, PANEL):
                cols[j] = cols[j] - coef * row(cols[j])
            left = left - coef * row(left)
            right = right - coef * row(right)
        left, right = left * scale, right * scale
        work[rows, :BASE] = left
        work[rows, BASE:] = right
        below = jnp.where(lane >= (p + 1) * PANEL, left, 0.0)
        both = jnp.concatenate([left, right], axis=1)
        work[...] = work[...] - lax.dot_general(
            below, both, (((0,), (0,)), ((), ())),
            precision=lax.Precision.HIGHEST, preferred_element_type=F32,
        )
        return carry

    lax.fori_loop(0, BASE // PANEL, panel, 0)


def ortho_kernel(total_cells, gram_ref, y_ref, basis_ref, factor_ref, full, work):
    width = factor_ref.shape[0]
    cw = width // CHUNKS
    count = width // BASE

    def dot(a, b, dims):
        return lax.dot_general(
            a, b, (dims, ((), ())), precision=lax.Precision.HIGHEST, preferred_element_type=F32
        )

    full[...] = jnp.zeros_like(full)
    for c in range(CHUNKS):
        for i in range(c + 1):
            place = c * (c + 1) // 2 + i
            full[i * cw:(i + 1) * cw, c * cw:(c + 1) * cw] = (
                gram_ref[place * cw:(place + 1) * cw] / jnp.float32(total_cells)
            )
    eye = (
        lax.broadcasted_iota(jnp.int32, (BASE, BASE), 0)
        == lax.broadcasted_iota(jnp.int32, (BASE, BASE), 1)
    ).astype(F32)
    for k in range(count):
        rows = slice(k * BASE, (k + 1) * BASE)
        full[rows, width + k * BASE:width + (k + 1) * BASE] = eye
        work[:, :BASE] = full[rows, rows]
        work[:, BASE:] = eye
        factor_block(work)
        full[rows, rows] = work[:, :BASE]
        mult = work[:, BASE:]
        beyond = slice((k + 1) * BASE, width + (k + 1) * BASE)
        new = dot(mult, full[rows, beyond], ((1,), (0,)))
        full[rows, beyond] = new
        for i in range(k + 1, count):
            here = slice(i * BASE, (i + 1) * BASE)
            span = slice(i * BASE, width + (k + 1) * BASE)
            full[here, span] = full[here, span] - dot(
                full[rows, here], full[rows, span], ((0,), (0,))
            )
    tri = lax.broadcasted_iota(jnp.int32, (width, width), 0) <= lax.broadcasted_iota(
        jnp.int32, (width, width), 1
    )
    factor_ref[...] = jnp.where(tri, full[:, :width], 0.0)
    ih, il = split(full[:, width:])

    def rows_of(n, carry):
        here = pl.ds(pl.multiple_of(n * 256, 256), 256)
        yh, yl = split(y_ref[here])

        def half(a, b):
            return lax.dot_general(a, b, (((1,), (1,)), ((), ())), preferred_element_type=F32)

        basis_ref[here] = half(yh, ih) + half(yh, il) + half(yl, ih)
        return carry

    lax.fori_loop(0, y_ref.shape[0] // 256, rows_of, 0)


def orthonormalize(gram, y, total_cells):
    width = y.shape[-1]
    return pl.pallas_call(
        functools.partial(ortho_kernel, total_cells),
        out_shape=(
            jax.ShapeDtypeStruct(y.shape, F32),
            jax.ShapeDtypeStruct((width, width), F32),
        ),
        in_specs=[pl.BlockSpec(memory_space=pltpu.VMEM)] * 2,
        out_specs=(pl.BlockSpec(memory_space=pltpu.VMEM),) * 2,
        scratch_shapes=[
            pltpu.VMEM((width, 2 * width), F32),
            pltpu.VMEM((BASE, 2 * BASE), F32),
        ],
        name="ortho",
    )(gram, y)


def body(ny, nz, initial_block, tile_ops, couple_ops, couple_map, cell_scale):
    shape = initial_block.shape
    tiles, cells, width = shape[2:]
    cw = width // CHUNKS
    packed = CHUNKS * (CHUNKS + 1) // 2 * cw
    stages = xor_stages(ny, nz, packed)
    ndir = 3 if nz == 2 else 4
    vm, any_ = pl.BlockSpec(memory_space=pltpu.VMEM), pl.BlockSpec(memory_space=pl.ANY)
    dma = pltpu.SemaphoreType.DMA
    y, gram = pl.pallas_call(
        functools.partial(filter_kernel, ny, nz, stages, width),
        out_shape=(
            jax.ShapeDtypeStruct((tiles, cells, width), F32),
            jax.ShapeDtypeStruct((packed, cw), F32),
        ),
        in_specs=[pl.BlockSpec(memory_space=pltpu.SMEM), vm, vm, any_, any_],
        out_specs=(vm, vm),
        scratch_shapes=[
            pltpu.VMEM((tiles, cells, cells), BF16),
            pltpu.VMEM((4, tiles, cells, cells), BF16),
            pltpu.VMEM((ROUNDS, CHUNKS, tiles, cells, cw), BF16),
            pltpu.VMEM((CHUNKS, tiles, cells, cw), F32),
            pltpu.VMEM((CHUNKS, tiles, cells, cw), F32),
            pltpu.VMEM((tiles * cells, width), BF16),
            pltpu.VMEM((tiles * cells, width), BF16),
            pltpu.VMEM((packed, cw), F32),
            pltpu.VMEM((packed, cw), F32),
            *[pltpu.VMEM((size // 2 if halve else size, cw), F32) for _, _, size, halve in stages],
            dma((2,)),
            dma((ndir, ROUNDS, CHUNKS)),
            dma((ndir, ROUNDS, CHUNKS)),
            dma((len(stages),)),
            dma((len(stages),)),
            dma((len(stages),)),
            dma((len(stages),)),
            *[pltpu.VMEM((tiles, cells, cw), BF16)] * (ndir * ROUNDS * CHUNKS),
        ],
        compiler_params=pltpu.CompilerParams(collective_id=0, has_side_effects=True),
        name="filter",
    )(couple_map[0, 0], cell_scale[0, 0][..., None], initial_block[0, 0], tile_ops[0, 0], couple_ops[0, 0])
    basis, factor = orthonormalize(gram, y.reshape(tiles * cells, width), tiles * cells * ny * nz)
    return basis.reshape(shape), factor


def solution(mesh):
    placed = (
        P("gy", "gz", None, None, None),
        P("gy", "gz", None, None, None),
        P("gy", "gz", None, None, None, None),
        P("gy", "gz", None, None),
        P("gy", "gz", None, None),
    )
    return jax.shard_map(
        functools.partial(body, mesh.shape["gy"], mesh.shape["gz"]),
        mesh=mesh,
        in_specs=placed,
        out_specs=(P("gy", "gz", None, None, None), P()),
        check_vma=False,
    )
```

```python
import functools

import jax
import jax.numpy as jnp
from jax import lax
from jax.experimental import pallas as pl
from jax.experimental.pallas import tpu as pltpu
from jax.sharding import PartitionSpec as P

F32, BF16 = jnp.float32, jnp.bfloat16
MESH = pl.DeviceIdType.MESH
ROUNDS = 3
CHUNKS = 2
BASE = 128
PANEL = 32


def split(x):
    hi = x.astype(BF16)
    return hi, (x - hi.astype(F32)).astype(BF16)


def packed(i, j):
    place = j * (j + 1) // 2 + i
    return slice(place * BASE, (place + 1) * BASE)


def xor_stages(ny, nz, rows):
    ybits = [("gy", b) for b in range(ny.bit_length() - 1)]
    zbits = [("gz", b) for b in range(nz.bit_length() - 1)]
    groups = [ybits[:1], zbits[:1] + ybits[1:2]]
    left = ybits[2:] + zbits[1:]
    groups += [left[n:n + 2] for n in range(0, len(left), 2)]
    stages, size = [], rows
    for group in groups:
        if size % (8 << len(group)) == 0:
            stages.append((tuple(group), size, True))
            size >>= len(group)
            continue
        for bit in group:
            halve = size % 16 == 0
            stages.append(((bit,), size, halve))
            size = size // 2 if halve else size
    return stages


def part_of(stage):
    bits, size, halve = stage
    return size >> len(bits) if halve else size


def filter_kernel(
    ny, nz, stages, nvec,
    map_ref, scale_row, first_ref, tile_hbm, couple_hbm,
    y_hbm, gram_ref,
    y_ref, scale_wide, tile_ref, couple_ref, sent, second, third, hi, lo, gsum, gall, *rest,
):
    peers = [(n, m) for n, stage in enumerate(stages) for m in range(1, 1 << len(stage[0]))]
    pieces, rest = dict(zip(peers, rest)), rest[len(peers):]
    index = {peer: k for k, peer in enumerate(peers)}
    op_sem, send_sem, recv_sem, rs_send, rs_recv, ag_send, ag_recv, *landed = rest
    got = {
        (d, r, c): landed[(d * ROUNDS + r) * CHUNKS + c]
        for d in range(len(landed) // (ROUNDS * CHUNKS)) for r in range(ROUNDS) for c in range(CHUNKS)
    }
    tiles, cells, width = first_ref.shape
    cw = width // CHUNKS
    iy, iz = lax.axis_index("gy"), lax.axis_index("gz")
    where = {"gy": iy, "gz": iz}

    def code_of(bits):
        return sum(((where[axis] // (2**bit)) % 2) * 2**k for k, (axis, bit) in enumerate(bits))

    def partner(bits, m):
        device, code = {}, 0
        for k, (axis, bit) in enumerate(bits):
            b = (where[axis] // (2**bit)) % 2
            if (m >> k) & 1:
                device[axis] = device.get(axis, where[axis]) + (1 - 2 * b) * (2**bit)
                b = 1 - b
            code = code + b * 2**k
        return device, code

    targets = [{"gy": (iy + 1) % ny}, {"gy": (iy + ny - 1) % ny}]
    if nz == 2:
        targets.append({"gz": 1 - iz})
        slot = (0, 1, 2, 2)
    else:
        targets += [{"gz": (iz + 1) % nz}, {"gz": (iz + nz - 1) % nz}]
        slot = (0, 1, 2, 3)

    copies_in = [
        pltpu.make_async_copy(tile_hbm, tile_ref, op_sem.at[0]),
        pltpu.make_async_copy(couple_hbm, couple_ref, op_sem.at[1]),
    ]
    for copy in copies_in:
        copy.start()

    barrier = pltpu.get_barrier_semaphore()
    greeted = targets + [partner(stages[n][0], m)[0] for n, m in peers]
    for other in greeted:
        pl.semaphore_signal(barrier, inc=1, device_id=other, device_id_type=MESH)

    def send(r, c):
        made = []
        for d, other in enumerate(targets):
            copy = pltpu.make_async_remote_copy(
                src_ref=sent.at[r, c],
                dst_ref=got[d, r, c],
                send_sem=send_sem.at[d, r, c],
                recv_sem=recv_sem.at[d, r, c],
                device_id=other,
                device_id_type=MESH,
            )
            copy.start()
            made.append(copy)
        return made

    for t in range(tiles):
        scale_wide[t] = jnp.broadcast_to(scale_row[t:t + 1, :], (BASE, cells)).T

    def scale_ref(t):
        return jnp.concatenate([scale_wide[t]] * (cw // BASE), axis=1)

    moving = {}
    for c in range(CHUNKS):
        for t in range(tiles):
            sent[0, c, t] = (scale_ref(t) * first_ref[t, :, c * cw:(c + 1) * cw].astype(F32)).astype(BF16)
        if c == 0:
            pl.semaphore_wait(barrier, len(greeted))
        moving[0, c] = send(0, c)
    for copy in copies_in:
        copy.wait()

    def gram_of(i, j):
        def dot(a, b):
            return lax.dot_general(a, b, (((0,), (0,)), ((), ())), preferred_element_type=F32)
        left, right = slice(i * cw, (i + 1) * cw), slice(j * cw, (j + 1) * cw)
        total = dot(hi[:, left], hi[:, right])
        total += dot(hi[:, left], lo[:, right])
        total += dot(lo[:, left], hi[:, right])
        per = cw // BASE
        for a in range(per):
            for b in range(per):
                if i * per + a <= j * per + b:
                    gsum[packed(i * per + a, j * per + b)] = total[
                        a * BASE:(a + 1) * BASE, b * BASE:(b + 1) * BASE
                    ]

    for r in range(ROUNDS):
        for c in range(CHUNKS):
            for copy in moving[r, c]:
                copy.wait_recv()
            cols = slice(c * cw, (c + 1) * cw)

            def one(t, carry, r=r, c=c, cols=cols):
                acc = jnp.dot(tile_ref[t], sent[r, c, t], preferred_element_type=F32)
                for d in range(4):
                    acc += jnp.dot(
                        couple_ref[d, t], got[slot[d], r, c][map_ref[d, t]], preferred_element_type=F32
                    )
                s = scale_ref(t)
                if r == 0:
                    y = first_ref[t, :, cols].astype(F32)
                elif r == 1:
                    y = second[c, t]
                else:
                    y = third[c, t]
                py = ((1.0 - 1.1) * y - s * acc) / 0.9
                if r == 0:
                    new = py
                    second[c, t] = new
                elif r == 1:
                    new = 2.0 * py - first_ref[t, :, cols].astype(F32)
                    third[c, t] = new
                else:
                    new = 2.0 * py - second[c, t]
                    y_ref[t, :, cols] = new
                    a, b = split(new)
                    here = pl.ds(pl.multiple_of(t * cells, cells), cells)
                    hi[here, cols] = a
                    lo[here, cols] = b
                if r < ROUNDS - 1:
                    sent[r + 1, c, t] = (s * new).astype(BF16)
                return carry

            lax.fori_loop(0, tiles, one, 0)
            if r < ROUNDS - 1:
                moving[r + 1, c] = send(r + 1, c)
            else:
                for i in range(c + 1):
                    gram_of(i, c)
    y_out = pltpu.make_async_copy(y_ref, y_hbm, op_sem.at[2])
    y_out.start()

    base = 0
    for n, (bits, size, halve) in enumerate(stages):
        part = part_of(stages[n])
        copies = []
        for m in range(1, 1 << len(bits)):
            other, code = partner(bits, m)
            start = base + code * part if halve else base
            copy = pltpu.make_async_remote_copy(
                src_ref=gsum.at[pl.ds(pl.multiple_of(start, 8), part)],
                dst_ref=pieces[n, m],
                send_sem=rs_send.at[index[n, m]],
                recv_sem=rs_recv.at[index[n, m]],
                device_id=other,
                device_id_type=MESH,
            )
            copy.start()
            copies.append(copy)
        for copy in copies:
            copy.wait()
        if halve:
            base = base + code_of(bits) * part
        here = pl.ds(pl.multiple_of(base, 8), part)
        total = gsum[here]
        for m in range(1, 1 << len(bits)):
            total = total + pieces[n, m][...]
        gsum[here] = total
    here = pl.ds(pl.multiple_of(base, 8), part_of(stages[-1]))
    gall[here] = gsum[here]
    for n in reversed(range(len(stages))):
        bits, size, halve = stages[n]
        if not halve:
            continue
        part = part_of(stages[n])
        here = pl.ds(pl.multiple_of(base, 8), part)
        copies = []
        for m in range(1, 1 << len(bits)):
            copy = pltpu.make_async_remote_copy(
                src_ref=gall.at[here],
                dst_ref=gall.at[here],
                send_sem=ag_send.at[index[n, m]],
                recv_sem=ag_recv.at[index[n, m]],
                device_id=partner(bits, m)[0],
                device_id_type=MESH,
            )
            copy.start()
            copies.append(copy)
        for copy in copies:
            copy.wait()
        base = base - code_of(bits) * part
    gram_ref[...] = gall[...]
    for made in moving.values():
        for copy in made:
            copy.wait_send()
    y_out.wait()


def factor_block(work):
    sub = lax.broadcasted_iota(jnp.int32, (PANEL, BASE), 0)
    lane = lax.broadcasted_iota(jnp.int32, (PANEL, BASE), 1)

    def panel(p, carry):
        rows = pl.ds(pl.multiple_of(p * PANEL, PANEL), PANEL)
        left, right = work[rows, :BASE], work[rows, BASE:]
        turned = pltpu.roll(left, lax.rem(BASE - p * PANEL, BASE), 1)
        cols = [jnp.broadcast_to(turned[:, j:j + 1], (PANEL, BASE)) for j in range(PANEL)]
        scale = jnp.zeros((PANEL, BASE), F32)
        for i in range(PANEL):
            def row(x):
                return jnp.broadcast_to(x[i:i + 1], (PANEL, BASE))
            inv = lax.rsqrt(row(cols[i]))
            coef = jnp.where(sub > i, cols[i] * (inv * inv), 0.0)
            scale = jnp.where(sub == i, inv, scale)
            for j in range(i + 1, PANEL):
                cols[j] = cols[j] - coef * row(cols[j])
            left = left - coef * row(left)
            right = right - coef * row(right)
        left, right = left * scale, right * scale
        work[rows, :BASE] = left
        work[rows, BASE:] = right
        below = jnp.where(lane >= (p + 1) * PANEL, left, 0.0)
        both = jnp.concatenate([left, right], axis=1)
        work[...] = work[...] - lax.dot_general(
            below, both, (((0,), (0,)), ((), ())),
            precision=lax.Precision.HIGHEST, preferred_element_type=F32,
        )
        return carry

    lax.fori_loop(0, BASE // PANEL, panel, 0)


def ortho_kernel(total_cells, gram_ref, y_hbm, basis_hbm, factor_ref, full, work, y_ref, basis_ref, y_sem, out_sem):
    width = factor_ref.shape[0]
    count = width // BASE
    y_in = pltpu.make_async_copy(y_hbm, y_ref, y_sem)
    y_in.start()

    def dot(a, b, dims):
        return lax.dot_general(
            a, b, (dims, ((), ())), precision=lax.Precision.HIGHEST, preferred_element_type=F32
        )

    full[...] = jnp.zeros_like(full)
    for j in range(count):
        for i in range(j + 1):
            full[i * BASE:(i + 1) * BASE, j * BASE:(j + 1) * BASE] = (
                gram_ref[packed(i, j)] / jnp.float32(total_cells)
            )
    eye = (
        lax.broadcasted_iota(jnp.int32, (BASE, BASE), 0)
        == lax.broadcasted_iota(jnp.int32, (BASE, BASE), 1)
    ).astype(F32)
    for k in range(count):
        rows = slice(k * BASE, (k + 1) * BASE)
        full[rows, width + k * BASE:width + (k + 1) * BASE] = eye
        work[:, :BASE] = full[rows, rows]
        work[:, BASE:] = eye
        factor_block(work)
        full[rows, rows] = work[:, :BASE]
        mult = work[:, BASE:]
        beyond = slice((k + 1) * BASE, width + (k + 1) * BASE)
        new = dot(mult, full[rows, beyond], ((1,), (0,)))
        full[rows, beyond] = new
        for i in range(k + 1, count):
            here = slice(i * BASE, (i + 1) * BASE)
            span = slice(i * BASE, width + (k + 1) * BASE)
            full[here, span] = full[here, span] - dot(
                full[rows, here], full[rows, span], ((0,), (0,))
            )
    tri = lax.broadcasted_iota(jnp.int32, (width, width), 0) <= lax.broadcasted_iota(
        jnp.int32, (width, width), 1
    )
    factor_ref[...] = jnp.where(tri, full[:, :width], 0.0)
    ih, il = split(full[:, width:])

    def half(a, b):
        return lax.dot_general(a, b, (((1,), (1,)), ((), ())), preferred_element_type=F32)

    y_in.wait()
    outs = []
    for n in range(y_ref.shape[0] // 256):
        here = pl.ds(n * 256, 256)
        yh, yl = split(y_ref[here])
        basis_ref[here] = half(yh, ih) + half(yh, il) + half(yl, ih)
        copy = pltpu.make_async_copy(basis_ref.at[here], basis_hbm.at[here], out_sem.at[n])
        copy.start()
        outs.append(copy)
    for copy in outs:
        copy.wait()


def orthonormalize(gram, y, total_cells):
    width = y.shape[-1]
    return pl.pallas_call(
        functools.partial(ortho_kernel, total_cells),
        out_shape=(
            jax.ShapeDtypeStruct(y.shape, F32),
            jax.ShapeDtypeStruct((width, width), F32),
        ),
        in_specs=[pl.BlockSpec(memory_space=pltpu.VMEM), pl.BlockSpec(memory_space=pl.ANY)],
        out_specs=(pl.BlockSpec(memory_space=pl.ANY), pl.BlockSpec(memory_space=pltpu.VMEM)),
        scratch_shapes=[
            pltpu.VMEM((width, 2 * width), F32),
            pltpu.VMEM((BASE, 2 * BASE), F32),
            pltpu.VMEM(y.shape, F32),
            pltpu.VMEM(y.shape, F32),
            pltpu.SemaphoreType.DMA,
            pltpu.SemaphoreType.DMA((y.shape[0] // 256,)),
        ],
        name="ortho",
    )(gram, y)


def body(ny, nz, initial_block, tile_ops, couple_ops, couple_map, cell_scale):
    shape = initial_block.shape
    tiles, cells, width = shape[2:]
    cw = width // CHUNKS
    count = width // BASE
    rows = count * (count + 1) // 2 * BASE
    stages = xor_stages(ny, nz, rows)
    parts = [part_of(stage) for stage in stages for _ in range(1, 1 << len(stage[0]))]
    ndir = 3 if nz == 2 else 4
    vm, any_ = pl.BlockSpec(memory_space=pltpu.VMEM), pl.BlockSpec(memory_space=pl.ANY)
    dma = pltpu.SemaphoreType.DMA
    y, gram = pl.pallas_call(
        functools.partial(filter_kernel, ny, nz, stages, width),
        out_shape=(
            jax.ShapeDtypeStruct((tiles, cells, width), F32),
            jax.ShapeDtypeStruct((rows, BASE), F32),
        ),
        in_specs=[pl.BlockSpec(memory_space=pltpu.SMEM), vm, vm, any_, any_],
        out_specs=(any_, vm),
        scratch_shapes=[
            pltpu.VMEM((tiles, cells, width), F32),
            pltpu.VMEM((tiles, cells, BASE), F32),
            pltpu.VMEM((tiles, cells, cells), BF16),
            pltpu.VMEM((4, tiles, cells, cells), BF16),
            pltpu.VMEM((ROUNDS, CHUNKS, tiles, cells, cw), BF16),
            pltpu.VMEM((CHUNKS, tiles, cells, cw), F32),
            pltpu.VMEM((CHUNKS, tiles, cells, cw), F32),
            pltpu.VMEM((tiles * cells, width), BF16),
            pltpu.VMEM((tiles * cells, width), BF16),
            pltpu.VMEM((rows, BASE), F32),
            pltpu.VMEM((rows, BASE), F32),
            *[pltpu.VMEM((part, BASE), F32) for part in parts],
            dma((3,)),
            dma((ndir, ROUNDS, CHUNKS)),
            dma((ndir, ROUNDS, CHUNKS)),
            dma((len(parts),)),
            dma((len(parts),)),
            dma((len(parts),)),
            dma((len(parts),)),
            *[pltpu.VMEM((tiles, cells, cw), BF16)] * (ndir * ROUNDS * CHUNKS),
        ],
        compiler_params=pltpu.CompilerParams(collective_id=0, has_side_effects=True),
        name="filter",
    )(couple_map[0, 0], cell_scale[0, 0], initial_block[0, 0], tile_ops[0, 0], couple_ops[0, 0])
    basis, factor = orthonormalize(gram, y.reshape(tiles * cells, width), tiles * cells * ny * nz)
    return basis.reshape(shape), factor


def solution(mesh):
    placed = (
        P("gy", "gz", None, None, None),
        P("gy", "gz", None, None, None),
        P("gy", "gz", None, None, None, None),
        P("gy", "gz", None, None),
        P("gy", "gz", None, None),
    )
    return jax.shard_map(
        functools.partial(body, mesh.shape["gy"], mesh.shape["gz"]),
        mesh=mesh,
        in_specs=placed,
        out_specs=(P("gy", "gz", None, None, None), P()),
        check_vma=False,
    )
```
